32 devices in a mesh: seq: 8 (over z, x), head: 4 (over y, core).
Axes of the slice: x: 2, y: 2, z: 4, core: 2. Of those that a mesh axis runs over, the one named last changes fastest.
Arguments:
- queries: bfloat16 [2048, 512], P('seq', 'head'), may hold values from -16 to 16
- keys: bfloat16 [2048, 512], P(('seq', 'head')), may hold values from -16 to 16
- values: bfloat16 [2048, 512], P(('seq', 'head')), may hold values from -6 to 6
- out_grad: bfloat16 [2048, 512], P('seq', 'head'), may hold values from -6 to 6
Outputs:
- attended: bfloat16 [2048, 512], P('seq', 'head')
- query_grad: float32 [2048, 512], P('seq', 'head')
- key_grad: float32 [2048, 512], P('seq', 'head')
- value_grad: float32 [2048, 512], P('seq', 'head')
The draws below stay inside these ranges and needn't reach their ends.
All inputs are finite; a program needn't handle non-finite values.
Results may differ from the reference program's by a relative error of at most 0.0095.
Values may be sent and summed in bfloat16 or wider, within the bound.
A program may use at most 64 MiB of HBM per device.

```python
import math
import jax
import jax.numpy as jnp
from jax import lax

HEAD_DIM = 128
HEADS = 4
TOKENS = 2048


def query_key_pair(key):
    columns = HEADS * HEAD_DIM
    query_base = jax.random.normal(jax.random.fold_in(key, 101), (TOKENS, columns), jnp.float32)
    key_base = jax.random.normal(jax.random.fold_in(key, 202), (TOKENS, columns), jnp.float32)
    query_out = query_base * 3.0
    key_out = key_base
    return (jnp.clip(query_out, -16.0, 16.0), jnp.clip(key_out, -16.0, 16.0))


def draw_queries(key, part):
    pair = query_key_pair(key)
    return pair[0].astype(jnp.bfloat16)


def draw_keys(key, part):
    pair = query_key_pair(key)
    return pair[1].astype(jnp.bfloat16)


def levels(stream_key, shape, cuts, least, high):
    gain, own = 1.0, jax.random.fold_in(stream_key, 6)
    for dim, shards_of in cuts:
        heights = jnp.exp(jax.random.uniform(jax.random.fold_in(own, dim), (shards_of,), jnp.float32, least / len(cuts), high / len(cuts)))
        gain = gain * jnp.repeat(heights, shape[dim] // shards_of).reshape([-1 if axis == dim else 1 for axis in range(len(shape))])
    return gain


def normal_values(stream_key, shape, width, reach, cuts=(), held_as=jnp.bfloat16):
    result = width * jax.random.normal(stream_key, shape, jnp.float32)
    if cuts:
        result = result * levels(stream_key, shape, cuts, -0.22, 0.18)
    return jnp.clip(result, -reach, reach).astype(held_as)


def setup_inputs(seed: int = 0) -> dict:
    streams_of = jax.random.split(jax.random.key(seed), 5)
    return {
        "queries": draw_queries(jax.random.fold_in(streams_of[4], 71), 0),
        "keys": draw_keys(jax.random.fold_in(streams_of[4], 71), 0),
        "values": normal_values(streams_of[2], (TOKENS, HEADS * HEAD_DIM), 1.0, 6.0, ((0, 32),)),
        "out_grad": normal_values(streams_of[3], (TOKENS, HEADS * HEAD_DIM), 1.0, 6.0, ((0, 8), (1, 4))),
    }


masked_value = -1e+30

def one_head(queries, keys, values, out_grad):
    length, head_width = queries.shape
    scaling = 1.0 / math.sqrt(head_width)
    span_rows = min(length, 512)
    span_count = length // span_rows
    key_pos = jnp.arange(length, dtype=jnp.int32)

    def forward(unused, number):
        qstart = (number * span_rows).astype(jnp.int32)
        query_piece = lax.dynamic_slice_in_dim(queries, qstart, span_rows, 0)
        query_pos = qstart + jnp.arange(span_rows, dtype=jnp.int32)
        allowed = key_pos[None, :] <= query_pos[:, None]
        scores = jnp.dot(query_piece, keys.T, preferred_element_type=jnp.float32) * scaling
        scores = jnp.where(allowed, scores, masked_value)
        rowmax = lax.optimization_barrier(jnp.max(scores, axis=1))
        weights = jnp.where(allowed, jnp.exp(scores - rowmax[:, None]), 0.0)
        rowsum = lax.optimization_barrier(jnp.sum(weights, axis=1))
        weighted = jnp.dot(weights.astype(jnp.bfloat16), values, preferred_element_type=jnp.float32)
        return (unused, (weighted / rowsum[:, None], rowmax + jnp.log(rowsum)))
    numbers = jnp.arange(span_count, dtype=jnp.int32)
    unused, (pieces, norms) = lax.scan(forward, jnp.zeros((), jnp.float32), numbers)
    output = pieces.reshape(length, head_width)
    log_norm = norms.reshape(length)
    row_delta = lax.optimization_barrier(jnp.sum(out_grad.astype(jnp.float32) * output, axis=1))

    def backward(running, number):
        key_total, value_total = running
        qstart = (number * span_rows).astype(jnp.int32)
        query_piece = lax.dynamic_slice_in_dim(queries, qstart, span_rows, 0)
        grad_piece = lax.dynamic_slice_in_dim(out_grad, qstart, span_rows, 0)
        norm_piece = lax.dynamic_slice_in_dim(log_norm, qstart, span_rows, 0)
        delta_piece = lax.dynamic_slice_in_dim(row_delta, qstart, span_rows, 0)
        query_pos = qstart + jnp.arange(span_rows, dtype=jnp.int32)
        allowed = key_pos[None, :] <= query_pos[:, None]
        scores = jnp.dot(query_piece, keys.T, preferred_element_type=jnp.float32) * scaling
        probs = jnp.where(allowed, jnp.exp(scores - norm_piece[:, None]), 0.0)
        grad_probs = jnp.dot(grad_piece, values.T, preferred_element_type=jnp.float32)
        grad_scores = (probs * (grad_probs - delta_piece[:, None]) * scaling).astype(jnp.bfloat16)
        query_part = jnp.dot(grad_scores, keys, preferred_element_type=jnp.float32)
        key_total = key_total + jnp.dot(grad_scores.T, query_piece, preferred_element_type=jnp.float32)
        value_total = value_total + jnp.dot(probs.astype(jnp.bfloat16).T, grad_piece, preferred_element_type=jnp.float32)
        return ((key_total, value_total), query_part)
    initial = (jnp.zeros((length, head_width), jnp.float32), jnp.zeros((length, head_width), jnp.float32))
    (key_grad, value_grad), query_parts = lax.scan(backward, initial, numbers)
    query_grad = query_parts.reshape(length, head_width)
    return (output.astype(jnp.bfloat16), query_grad, key_grad, value_grad)

def reference(queries, keys, values, out_grad):
    outputs = []
    for head_number in range(HEADS):
        low_col = head_number * HEAD_DIM
        results = one_head(queries[:, low_col:low_col + HEAD_DIM], keys[:, low_col:low_col + HEAD_DIM], values[:, low_col:low_col + HEAD_DIM], out_grad[:, low_col:low_col + HEAD_DIM])
        outputs.append(results)
    attended = jnp.concatenate([item[0] for item in outputs], axis=1)
    query_grad = jnp.concatenate([item[1] for item in outputs], axis=1)
    key_grad = jnp.concatenate([item[2] for item in outputs], axis=1)
    value_grad = jnp.concatenate([item[3] for item in outputs], axis=1)
    return (attended, query_grad, key_grad, value_grad)
```

```python
import functools
import math

import jax
import jax.numpy as jnp
from jax import lax
from jax.experimental import pallas as pl
from jax.experimental.pallas import tpu as pltpu
from jax.sharding import PartitionSpec as P

MESH = pl.DeviceIdType.MESH
masked_value = -1e30
NT = (((1,), (1,)), ((), ()))
NN = (((1,), (0,)), ((), ()))


def dot(a, b, dims):
    return lax.dot_general(a, b, dims, preferred_element_type=jnp.float32)


def row_width(shards):
    width = max(1, math.isqrt(shards // 2))
    while shards % width:
        width -= 1
    return width


def kernel(
    S, X, H, scaling,
    q_ref, k_ref, v_ref, g_ref,
    att_ref, dq_ref, dk_ref, dv_ref,
    kv, qd, stats, acc, top, total,
    local_sem, swap_send, swap_recv, up_send, side_send, block_recv, stat_send, stat_recv,
):
    Z = S // X
    rows, width = q_ref.shape
    part = k_ref.shape[0]
    me, head = lax.axis_index("seq"), lax.axis_index("head")
    z, x = lax.div(me, X), lax.rem(me, X)

    own_rows = pl.ds(pl.multiple_of(head * part, part), part)

    def columns(number):
        return pl.ds(pl.multiple_of(number * width, width), width)

    local = [
        pltpu.make_async_copy(q_ref, qd.at[me, 0], local_sem.at[0]),
        pltpu.make_async_copy(g_ref, qd.at[me, 1], local_sem.at[1]),
        pltpu.make_async_copy(k_ref.at[:, columns(head)], kv.at[me, 0, own_rows], local_sem.at[2]),
        pltpu.make_async_copy(v_ref.at[:, columns(head)], kv.at[me, 1, own_rows], local_sem.at[3]),
    ]
    for copy in local:
        copy.start()

    barrier = pltpu.get_barrier_semaphore()
    for step in range(1, S):
        pl.semaphore_signal(
            barrier, inc=1, device_id={"seq": lax.rem(me + step, S)}, device_id_type=MESH
        )
    for step in range(1, H):
        pl.semaphore_signal(
            barrier, inc=1, device_id={"head": lax.rem(head + step, H)}, device_id_type=MESH
        )
    pl.semaphore_wait(barrier, S + H - 2)

    swaps = []
    for step in range(1, H):
        other = lax.rem(head + step, H)
        for kind, ref in enumerate((k_ref, v_ref)):
            swaps.append(
                pltpu.make_async_remote_copy(
                    src_ref=ref.at[:, columns(other)],
                    dst_ref=kv.at[me, kind, own_rows],
                    send_sem=swap_send.at[kind, step],
                    recv_sem=swap_recv.at[kind, step],
                    device_id={"head": other},
                    device_id_type=MESH,
                )
            )
    for copy in swaps:
        copy.start()

    buffers = (kv, qd)

    def along(kind, t):
        zb = z - t if kind == 0 else z + t
        b = zb * X + x
        target = me + X if kind == 0 else me - X
        needed = (z < Z - 1) if kind == 0 else (z > 0)
        copy = pltpu.make_async_remote_copy(
            src_ref=buffers[kind].at[b],
            dst_ref=buffers[kind].at[b],
            send_sem=up_send.at[kind, t],
            recv_sem=block_recv.at[kind, b],
            device_id={"seq": target},
            device_id_type=MESH,
        )
        return needed, copy

    def beside(kind, t, step):
        zb = z - t if kind == 0 else z + t
        b = zb * X + x
        other = lax.rem(x + step, X)
        needed = (t > 0) | ((other > x) if kind == 0 else (other < x))
        copy = pltpu.make_async_remote_copy(
            src_ref=buffers[kind].at[b],
            dst_ref=buffers[kind].at[b],
            send_sem=side_send.at[kind, t, step],
            recv_sem=block_recv.at[kind, b],
            device_id={"seq": z * X + other},
            device_id_type=MESH,
        )
        return needed, copy

    def outgoing(kind, t):
        return [along(kind, t)] + [beside(kind, t, step) for step in range(1, X)]

    def send_on(kind, t):
        for needed, copy in outgoing(kind, t):
            @pl.when(needed)
            def _(copy=copy):
                copy.start()

    def arrived(kind, b):
        pltpu.make_async_copy(
            buffers[kind].at[b], buffers[kind].at[b], block_recv.at[kind, b]
        ).wait()

    local[0].wait()
    local[1].wait()
    send_on(1, 0)
    for copy in local[2:]:
        copy.wait()
    for copy in swaps:
        copy.wait_recv()
    send_on(0, 0)

    def forward(b, diagonal):
        s = dot(qd[me, 0], kv[b, 0], NT) * scaling
        if diagonal:
            r = lax.broadcasted_iota(jnp.int32, (rows, rows), 0)
            c = lax.broadcasted_iota(jnp.int32, (rows, rows), 1)
            s = jnp.where(c <= r, s, masked_value)
            high = jnp.max(s, axis=1, keepdims=True)
        else:
            old = top[:, :1]
            high = jnp.maximum(old, jnp.max(s, axis=1, keepdims=True))
        p = jnp.exp(s - high)
        psum = jnp.sum(p, axis=1, keepdims=True)
        pv = dot(p.astype(jnp.bfloat16), kv[b, 1], NN)
        if diagonal:
            total[...] = jnp.broadcast_to(psum, total.shape)
            acc[...] = pv
        else:
            factor = jnp.exp(old - high)
            total[...] = total[...] * factor + psum
            acc[...] = acc[...] * factor + pv
        top[...] = jnp.broadcast_to(high, top.shape)

    forward(me, True)

    def relay(t, carry):
        up = z - t >= 0
        down = z + t < Z

        @pl.when(up)
        def _():
            arrived(0, (z - t) * X + x)
            send_on(0, t)

        @pl.when(down)
        def _():
            arrived(1, (z + t) * X + x)
            send_on(1, t)

        @pl.when(up)
        def _():
            forward((z - t) * X + x, False)

        for step in range(1, X):
            other = lax.rem(x + step, X)

            @pl.when((z - (t - 1) >= 0) & ((t > 1) | (other < x)))
            def _(other=other):
                b = (z - (t - 1)) * X + other
                arrived(0, b)
                forward(b, False)

        return carry

    lax.fori_loop(1, Z + 1, relay, 0)

    sums = total[:, :1]
    output = acc[...] / sums
    att_ref[...] = output.astype(att_ref.dtype)
    log_norm = top[:, :1] + jnp.log(sums)
    delta = jnp.sum(qd[me, 1].astype(jnp.float32) * output, axis=1, keepdims=True)
    top[...] = jnp.broadcast_to(log_norm, top.shape)
    total[...] = jnp.broadcast_to(delta, total.shape)
    stats[me, 0:4, :] = top[...].T[0:4]
    stats[me, 4:8, :] = total[...].T[0:4]

    def stat_copy(b):
        return pltpu.make_async_remote_copy(
            src_ref=stats.at[me],
            dst_ref=stats.at[me],
            send_sem=stat_send.at[b],
            recv_sem=stat_recv.at[me],
            device_id={"seq": b},
            device_id_type=MESH,
        )

    def stat_out(b, carry):
        stat_copy(b).start()
        return carry

    lax.fori_loop(0, me, stat_out, 0)

    def query_side(b, diagonal):
        s = dot(qd[me, 0], kv[b, 0], NT) * scaling
        p = jnp.exp(s - top[:, :1])
        if diagonal:
            r = lax.broadcasted_iota(jnp.int32, (rows, rows), 0)
            c = lax.broadcasted_iota(jnp.int32, (rows, rows), 1)
            p = jnp.where(c <= r, p, 0.0)
        gp = dot(qd[me, 1], kv[b, 1], NT)
        gs = (p * (gp - total[:, :1]) * scaling).astype(jnp.bfloat16)
        return dot(gs, kv[b, 0], NN)

    dq_ref[...] = query_side(me, True)

    def query_step(b, carry):
        dq_ref[...] += query_side(b, False)
        return carry

    lax.fori_loop(0, me, query_step, 0)

    def key_side(b, diagonal):
        s = dot(kv[me, 0], qd[b, 0], NT) * scaling
        p = jnp.exp(s - stats[b, 0:1, :])
        if diagonal:
            r = lax.broadcasted_iota(jnp.int32, (rows, rows), 0)
            c = lax.broadcasted_iota(jnp.int32, (rows, rows), 1)
            p = jnp.where(r <= c, p, 0.0)
        gp = dot(kv[me, 1], qd[b, 1], NT)
        gs = (p * (gp - stats[b, 4:5, :]) * scaling).astype(jnp.bfloat16)
        return dot(gs, qd[b, 0], NN), dot(p.astype(jnp.bfloat16), qd[b, 1], NN)

    dk, dv = key_side(me, True)
    dk_ref[...] = dk
    dv_ref[...] = dv

    def key_step(b, carry):
        @pl.when(lax.rem(b, X) != x)
        def _():
            arrived(1, b)

        pltpu.make_async_copy(stats.at[b], stats.at[b], stat_recv.at[b]).wait()
        dk, dv = key_side(b, False)
        dk_ref[...] += dk
        dv_ref[...] += dv
        return carry

    lax.fori_loop(me + 1, S, key_step, 0)

    for copy in swaps:
        copy.wait_send()

    def drain(t, carry):
        for kind in range(2):
            present = (z - t >= 0) if kind == 0 else (z + t < Z)
            for needed, copy in outgoing(kind, t):
                @pl.when(present & needed)
                def _(copy=copy):
                    copy.wait_send()
        return carry

    lax.fori_loop(0, Z, drain, 0)

    def stat_drain(b, carry):
        stat_copy(b).wait_send()
        return carry

    lax.fori_loop(0, me, stat_drain, 0)


def solution(mesh):
    S, H = mesh.shape["seq"], mesh.shape["head"]
    X = row_width(S)
    Z = S // X

    def step(queries, keys, values, out_grad):
        rows, width = queries.shape
        f32 = jax.ShapeDtypeStruct((rows, width), jnp.float32)
        DMA = pltpu.SemaphoreType.DMA
        return pl.pallas_call(
            functools.partial(kernel, S, X, H, 1.0 / math.sqrt(width)),
            out_shape=(jax.ShapeDtypeStruct((rows, width), jnp.bfloat16), f32, f32, f32),
            in_specs=[pl.BlockSpec(memory_space=pl.ANY)] * 4,
            out_specs=(pl.BlockSpec(memory_space=pltpu.VMEM),) * 4,
            scratch_shapes=[
                pltpu.VMEM((S, 2, rows, width), jnp.bfloat16),
                pltpu.VMEM((S, 2, rows, width), jnp.bfloat16),
                pltpu.VMEM((S, 8, rows), jnp.float32),
                pltpu.VMEM((rows, width), jnp.float32),
                pltpu.VMEM((rows, 128), jnp.float32),
                pltpu.VMEM((rows, 128), jnp.float32),
                DMA((4,)),
                DMA((2, H)),
                DMA((2, H)),
                DMA((2, Z)),
                DMA((2, Z, X)),
                DMA((2, S)),
                DMA((S,)),
                DMA((S,)),
            ],
            compiler_params=pltpu.CompilerParams(collective_id=0, has_side_effects=True),
            name="ring_attention",
        )(queries, keys, values, out_grad)

    return jax.shard_map(
        step,
        mesh=mesh,
        in_specs=(
            P("seq", "head"),
            P(("seq", "head"), None),
            P(("seq", "head"), None),
            P("seq", "head"),
        ),
        out_specs=(P("seq", "head"),) * 4,
        check_vma=False,
    )
```

```python
import functools
import math

import jax
import jax.numpy as jnp
from jax import lax
from jax.experimental import pallas as pl
from jax.experimental.pallas import tpu as pltpu
from jax.sharding import PartitionSpec as P

MESH = pl.DeviceIdType.MESH
masked_value = -1e30
NT = (((1,), (1,)), ((), ()))
NN = (((1,), (0,)), ((), ()))


def dot(a, b, dims):
    return lax.dot_general(a, b, dims, preferred_element_type=jnp.float32)


def row_width(shards):
    width = max(1, math.isqrt(shards // 2))
    while shards % width:
        width -= 1
    return width


def partner(head, step, count):
    if count & (count - 1):
        return lax.rem(step + count - head, count)
    other, bit = 0, 1
    while bit < count:
        other = other + bit * lax.rem(lax.div(head, bit) + step // bit, 2)
        bit *= 2
    return other


def kernel(
    S, X, H, scaling,
    q_ref, k_ref, v_ref, g_ref,
    att_ref, dq_ref, dk_ref, dv_ref,
    kv, qd, stats, acc, top, total,
    local_sem, swap_send, swap_recv, up_send, side_send, block_recv, stat_send, stat_recv,
):
    Z = S // X
    rows, width = q_ref.shape
    part = k_ref.shape[0]
    me, head = lax.axis_index("seq"), lax.axis_index("head")
    z, x = lax.div(me, X), lax.rem(me, X)

    own_rows = pl.ds(pl.multiple_of(head * part, part), part)

    def columns(number):
        return pl.ds(pl.multiple_of(number * width, width), width)

    local = [
        pltpu.make_async_copy(q_ref, qd.at[me, 0], local_sem.at[0]),
        pltpu.make_async_copy(g_ref, qd.at[me, 1], local_sem.at[1]),
        pltpu.make_async_copy(k_ref.at[:, columns(head)], kv.at[me, 0, own_rows], local_sem.at[2]),
        pltpu.make_async_copy(v_ref.at[:, columns(head)], kv.at[me, 1, own_rows], local_sem.at[3]),
    ]
    for copy in local:
        copy.start()

    barrier = pltpu.get_barrier_semaphore()
    above, below = z < Z - 1, z > 0
    for there, target in ((above, me + X), (below, me - X)):
        @pl.when(there)
        def _(target=target):
            pl.semaphore_signal(barrier, inc=1, device_id={"seq": target}, device_id_type=MESH)
    for step in range(1, X):
        pl.semaphore_signal(
            barrier, inc=1, device_id={"seq": z * X + lax.rem(x + step, X)}, device_id_type=MESH
        )
    for step in range(1, H):
        pl.semaphore_signal(
            barrier, inc=1, device_id={"head": partner(head, step, H)}, device_id_type=MESH
        )
    peers = X + H - 2 + lax.convert_element_type(above, jnp.int32)
    pl.semaphore_wait(barrier, peers + lax.convert_element_type(below, jnp.int32))

    swaps = []
    for step in range(1, H):
        other = partner(head, step, H)
        for kind, ref in enumerate((k_ref, v_ref)):
            swaps.append(
                pltpu.make_async_remote_copy(
                    src_ref=ref.at[:, columns(other)],
                    dst_ref=kv.at[me, kind, own_rows],
                    send_sem=swap_send.at[kind, step],
                    recv_sem=swap_recv.at[kind, step],
                    device_id={"head": other},
                    device_id_type=MESH,
                )
            )
    for copy in swaps:
        copy.start()

    buffers = (kv, qd)

    def piece(kind, b, step):
        start = pl.multiple_of(partner(head, step, H) * part, part)
        return buffers[kind].at[b, :, pl.ds(start, part)]

    def outgoing(kind, t, c):
        zb = z - t if kind == 0 else z + t
        b = zb * X + x
        chunk = piece(kind, b, c)

        def copy_to(target, send_sem):
            return pltpu.make_async_remote_copy(
                src_ref=chunk,
                dst_ref=chunk,
                send_sem=send_sem,
                recv_sem=block_recv.at[kind, b, c],
                device_id={"seq": target},
                device_id_type=MESH,
            )

        copies = [
            (
                above if kind == 0 else below,
                copy_to(me + X if kind == 0 else me - X, up_send.at[kind, t, c]),
            )
        ]
        for step in range(1, X):
            other = lax.rem(x + step, X)
            needed = (t > 0) | ((other > x) if kind == 0 else (other < x))
            copies.append((needed, copy_to(z * X + other, side_send.at[kind, t, step, c])))
        return copies

    def send_on(kind, t, c):
        for needed, copy in outgoing(kind, t, c):
            @pl.when(needed)
            def _(copy=copy):
                copy.start()

    def arrived(kind, b, c):
        chunk = piece(kind, b, c)
        pltpu.make_async_copy(chunk, chunk, block_recv.at[kind, b, c]).wait()

    def all_arrived(kind, b):
        for c in range(H):
            arrived(kind, b, c)

    local[2].wait()
    local[3].wait()
    send_on(0, 0, 0)
    local[0].wait()
    local[1].wait()
    for c in range(H):
        send_on(1, 0, c)
    for c in range(1, H):
        swaps[2 * c - 2].wait_recv()
        swaps[2 * c - 1].wait_recv()
        send_on(0, 0, c)

    def forward(b, diagonal):
        s = dot(qd[me, 0], kv[b, 0], NT) * scaling
        if diagonal:
            r = lax.broadcasted_iota(jnp.int32, (rows, rows), 0)
            c = lax.broadcasted_iota(jnp.int32, (rows, rows), 1)
            s = jnp.where(c <= r, s, masked_value)
            high = jnp.max(s, axis=1, keepdims=True)
        else:
            old = top[:, :1]
            high = jnp.maximum(old, jnp.max(s, axis=1, keepdims=True))
        p = jnp.exp(s - high)
        psum = jnp.sum(p, axis=1, keepdims=True)
        pv = dot(p.astype(jnp.bfloat16), kv[b, 1], NN)
        if diagonal:
            total[...] = jnp.broadcast_to(psum, total.shape)
            acc[...] = pv
        else:
            factor = jnp.exp(old - high)
            total[...] = total[...] * factor + psum
            acc[...] = acc[...] * factor + pv
        top[...] = jnp.broadcast_to(high, top.shape)

    forward(me, True)

    def relay(t, carry):
        up = z - t >= 0
        down = z + t < Z

        for c in range(H):
            @pl.when(up)
            def _():
                arrived(0, (z - t) * X + x, c)
                send_on(0, t, c)

            @pl.when(down)
            def _():
                arrived(1, (z + t) * X + x, c)
                send_on(1, t, c)

        @pl.when(up)
        def _():
            forward((z - t) * X + x, False)

        for step in range(1, X):
            other = lax.rem(x + step, X)

            @pl.when((z - (t - 1) >= 0) & ((t > 1) | (other < x)))
            def _(other=other):
                b = (z - (t - 1)) * X + other
                all_arrived(0, b)
                forward(b, False)

        return carry

    lax.fori_loop(1, Z + 1, relay, 0)

    sums = total[:, :1]
    output = acc[...] / sums
    att_ref[...] = output.astype(att_ref.dtype)
    log_norm = top[:, :1] + jnp.log(sums)
    delta = jnp.sum(qd[me, 1].astype(jnp.float32) * output, axis=1, keepdims=True)
    top[...] = jnp.broadcast_to(log_norm, top.shape)
    total[...] = jnp.broadcast_to(delta, total.shape)
    stats[me, 0:4, :] = top[...].T[0:4]
    stats[me, 4:8, :] = total[...].T[0:4]

    def stat_copy(b):
        return pltpu.make_async_remote_copy(
            src_ref=stats.at[me],
            dst_ref=stats.at[me],
            send_sem=stat_send.at[b],
            recv_sem=stat_recv.at[me],
            device_id={"seq": b},
            device_id_type=MESH,
        )

    def stat_out(b, carry):
        stat_copy(b).start()
        return carry

    lax.fori_loop(0, me, stat_out, 0)

    def query_side(b, diagonal):
        s = dot(qd[me, 0], kv[b, 0], NT) * scaling
        p = jnp.exp(s - top[:, :1])
        if diagonal:
            r = lax.broadcasted_iota(jnp.int32, (rows, rows), 0)
            c = lax.broadcasted_iota(jnp.int32, (rows, rows), 1)
            p = jnp.where(c <= r, p, 0.0)
        gp = dot(qd[me, 1], kv[b, 1], NT)
        gs = (p * (gp - total[:, :1]) * scaling).astype(jnp.bfloat16)
        return dot(gs, kv[b, 0], NN)

    dq_ref[...] = query_side(me, True)

    def query_step(b, carry):
        dq_ref[...] += query_side(b, False)
        return carry

    lax.fori_loop(0, me, query_step, 0)

    def key_side(b, diagonal):
        s = dot(kv[me, 0], qd[b, 0], NT) * scaling
        p = jnp.exp(s - stats[b, 0:1, :])
        if diagonal:
            r = lax.broadcasted_iota(jnp.int32, (rows, rows), 0)
            c = lax.broadcasted_iota(jnp.int32, (rows, rows), 1)
            p = jnp.where(r <= c, p, 0.0)
        gp = dot(kv[me, 1], qd[b, 1], NT)
        gs = (p * (gp - stats[b, 4:5, :]) * scaling).astype(jnp.bfloat16)
        return dot(gs, qd[b, 0], NN), dot(p.astype(jnp.bfloat16), qd[b, 1], NN)

    dk, dv = key_side(me, True)
    dk_ref[...] = dk
    dv_ref[...] = dv

    def key_step(b, carry):
        @pl.when(lax.rem(b, X) != x)
        def _():
            all_arrived(1, b)

        pltpu.make_async_copy(stats.at[b], stats.at[b], stat_recv.at[b]).wait()
        dk, dv = key_side(b, False)
        dk_ref[...] += dk
        dv_ref[...] += dv
        return carry

    lax.fori_loop(me + 1, S, key_step, 0)

    for copy in swaps:
        copy.wait_send()

    def drain(t, carry):
        for kind in range(2):
            present = (z - t >= 0) if kind == 0 else (z + t < Z)
            for c in range(H):
                for needed, copy in outgoing(kind, t, c):
                    @pl.when(present & needed)
                    def _(copy=copy):
                        copy.wait_send()
        return carry

    lax.fori_loop(0, Z, drain, 0)

    def stat_drain(b, carry):
        stat_copy(b).wait_send()
        return carry

    lax.fori_loop(0, me, stat_drain, 0)


def solution(mesh):
    S, H = mesh.shape["seq"], mesh.shape["head"]
    X = row_width(S)
    Z = S // X

    def step(queries, keys, values, out_grad):
        rows, width = queries.shape
        f32 = jax.ShapeDtypeStruct((rows, width), jnp.float32)
        DMA = pltpu.SemaphoreType.DMA
        return pl.pallas_call(
            functools.partial(kernel, S, X, H, 1.0 / math.sqrt(width)),
            out_shape=(jax.ShapeDtypeStruct((rows, width), jnp.bfloat16), f32, f32, f32),
            in_specs=[pl.BlockSpec(memory_space=pl.ANY)] * 4,
            out_specs=(pl.BlockSpec(memory_space=pltpu.VMEM),) * 4,
            scratch_shapes=[
                pltpu.VMEM((S, 2, rows, width), jnp.bfloat16),
                pltpu.VMEM((S, 2, rows, width), jnp.bfloat16),
                pltpu.VMEM((S, 8, rows), jnp.float32),
                pltpu.VMEM((rows, width), jnp.float32),
                pltpu.VMEM((rows, 128), jnp.float32),
                pltpu.VMEM((rows, 128), jnp.float32),
                DMA((4,)),
                DMA((2, H)),
                DMA((2, H)),
                DMA((2, Z, H)),
                DMA((2, Z, X, H)),
                DMA((2, S, H)),
                DMA((S,)),
                DMA((S,)),
            ],
            compiler_params=pltpu.CompilerParams(collective_id=0, has_side_effects=True),
            name="ring_attention",
        )(queries, keys, values, out_grad)

    return jax.shard_map(
        step,
        mesh=mesh,
        in_specs=(
            P("seq", "head"),
            P(("seq", "head"), None),
            P(("seq", "head"), None),
            P("seq", "head"),
        ),
        out_specs=(P("seq", "head"),) * 4,
        check_vma=False,
    )
```

```python
import functools
import math

import jax
import jax.numpy as jnp
from jax import lax
from jax.experimental import pallas as pl
from jax.experimental.pallas import tpu as pltpu
from jax.sharding import PartitionSpec as P

MESH = pl.DeviceIdType.MESH
masked_value = -1e30
NT = (((1,), (1,)), ((), ()))
NN = (((1,), (0,)), ((), ()))


def dot(a, b, dims):
    return lax.dot_general(a, b, dims, preferred_element_type=jnp.float32)


def row_width(shards):
    width = max(1, math.isqrt(shards // 2))
    while shards % width:
        width -= 1
    return width


def partner(head, step, count):
    if count & (count - 1):
        return lax.rem(step + count - head, count)
    other, bit = 0, 1
    while bit < count:
        other = other + bit * lax.rem(lax.div(head, bit) + step // bit, 2)
        bit *= 2
    return other


def kernel(
    S, X, H, scaling,
    q_ref, k_ref, v_ref, g_ref,
    att_ref, dq_ref, dk_ref, dv_ref,
    kv, qd, stats, acc, top, total,
    local_sem, swap_send, swap_recv, up_send, side_send, block_recv, stat_send, stat_recv,
):
    Z = S // X
    rows, width = q_ref.shape
    part = k_ref.shape[0]
    me, head = lax.axis_index("seq"), lax.axis_index("head")
    z, x = lax.div(me, X), lax.rem(me, X)

    own_rows = pl.ds(pl.multiple_of(head * part, part), part)

    def columns(number):
        return pl.ds(pl.multiple_of(number * width, width), width)

    local = [
        pltpu.make_async_copy(q_ref, qd.at[me, 0], local_sem.at[0]),
        pltpu.make_async_copy(g_ref, qd.at[me, 1], local_sem.at[1]),
        pltpu.make_async_copy(k_ref.at[:, columns(head)], kv.at[me, 0, own_rows], local_sem.at[2]),
        pltpu.make_async_copy(v_ref.at[:, columns(head)], kv.at[me, 1, own_rows], local_sem.at[3]),
    ]
    for copy in local:
        copy.start()

    barrier = pltpu.get_barrier_semaphore()
    above, below = z < Z - 1, z > 0
    for there, target in ((above, me + X), (below, me - X)):
        @pl.when(there)
        def _(target=target):
            pl.semaphore_signal(barrier, inc=1, device_id={"seq": target}, device_id_type=MESH)
    for step in range(1, X):
        pl.semaphore_signal(
            barrier, inc=1, device_id={"seq": z * X + lax.rem(x + step, X)}, device_id_type=MESH
        )
    for step in range(1, H):
        pl.semaphore_signal(
            barrier, inc=1, device_id={"head": partner(head, step, H)}, device_id_type=MESH
        )
    peers = X + H - 2 + lax.convert_element_type(above, jnp.int32)
    pl.semaphore_wait(barrier, peers + lax.convert_element_type(below, jnp.int32))

    swaps = []
    for step in range(1, H):
        other = partner(head, step, H)
        for kind, ref in enumerate((k_ref, v_ref)):
            swaps.append(
                pltpu.make_async_remote_copy(
                    src_ref=ref.at[:, columns(other)],
                    dst_ref=kv.at[me, kind, own_rows],
                    send_sem=swap_send.at[kind, step],
                    recv_sem=swap_recv.at[kind, step],
                    device_id={"head": other},
                    device_id_type=MESH,
                )
            )
    for copy in swaps:
        copy.start()

    buffers = (kv, qd)

    def piece(kind, b, step):
        start = pl.multiple_of(partner(head, step, H) * part, part)
        return buffers[kind].at[b, :, pl.ds(start, part)]

    def outgoing(kind, t, c):
        zb = z - t if kind == 0 else z + t
        b = zb * X + x
        chunk = piece(kind, b, c)

        def copy_to(target, send_sem):
            return pltpu.make_async_remote_copy(
                src_ref=chunk,
                dst_ref=chunk,
                send_sem=send_sem,
                recv_sem=block_recv.at[kind, b, c],
                device_id={"seq": target},
                device_id_type=MESH,
            )

        copies = [
            (
                above if kind == 0 else below,
                copy_to(me + X if kind == 0 else me - X, up_send.at[kind, t, c]),
            )
        ]
        for step in range(1, X):
            other = lax.rem(x + step, X)
            needed = (t > 0) | ((other > x) if kind == 0 else (other < x))
            copies.append((needed, copy_to(z * X + other, side_send.at[kind, t, step, c])))
        return copies

    def send_on(kind, t, c):
        for needed, copy in outgoing(kind, t, c):
            @pl.when(needed)
            def _(copy=copy):
                copy.start()

    def arrived(kind, b, c):
        chunk = piece(kind, b, c)
        pltpu.make_async_copy(chunk, chunk, block_recv.at[kind, b, c]).wait()

    def all_arrived(kind, b):
        for c in range(H):
            arrived(kind, b, c)

    local[2].wait()
    local[3].wait()
    send_on(0, 0, 0)
    local[0].wait()
    local[1].wait()
    for c in range(H):
        send_on(1, 0, c)
    for c in range(1, H):
        swaps[2 * c - 2].wait_recv()
        swaps[2 * c - 1].wait_recv()
        send_on(0, 0, c)

    def forward(b, diagonal):
        s = dot(qd[me, 0], kv[b, 0], NT) * scaling
        if diagonal:
            r = lax.broadcasted_iota(jnp.int32, (rows, rows), 0)
            c = lax.broadcasted_iota(jnp.int32, (rows, rows), 1)
            s = jnp.where(c <= r, s, masked_value)
            high = jnp.max(s, axis=1, keepdims=True)
        else:
            old = top[:, :1]
            high = jnp.maximum(old, jnp.max(s, axis=1, keepdims=True))
        p = jnp.exp(s - high)
        psum = jnp.sum(p, axis=1, keepdims=True)
        pv = dot(p.astype(jnp.bfloat16), kv[b, 1], NN)
        if diagonal:
            total[...] = jnp.broadcast_to(psum, total.shape)
            acc[...] = pv
        else:
            factor = jnp.exp(old - high)
            total[...] = total[...] * factor + psum
            acc[...] = acc[...] * factor + pv
        top[...] = jnp.broadcast_to(high, top.shape)

    forward(me, True)

    def relay(t, carry):
        up = z - t >= 0
        down = z + t < Z

        for c in range(H):
            @pl.when(up)
            def _():
                arrived(0, (z - t) * X + x, c)
                send_on(0, t, c)

            @pl.when(down)
            def _():
                arrived(1, (z + t) * X + x, c)
                send_on(1, t, c)

        @pl.when(up)
        def _():
            forward((z - t) * X + x, False)

        for step in range(1, X):
            other = lax.rem(x + step, X)

            @pl.when((z - (t - 1) >= 0) & ((t > 1) | (other < x)))
            def _(other=other):
                b = (z - (t - 1)) * X + other
                all_arrived(0, b)
                forward(b, False)

        return carry

    lax.fori_loop(1, Z + 1, relay, 0)

    sums = total[:, :1]
    output = acc[...] / sums
    att_ref[...] = output.astype(att_ref.dtype)
    log_norm = top[:, :1] + jnp.log(sums)
    delta = jnp.sum(qd[me, 1].astype(jnp.float32) * output, axis=1, keepdims=True)
    top[...] = jnp.broadcast_to(log_norm, top.shape)
    total[...] = jnp.broadcast_to(delta, total.shape)
    stats[me, 0:4, :] = top[...].T[0:4]
    stats[me, 4:8, :] = total[...].T[0:4]

    def stat_copy(b):
        return pltpu.make_async_remote_copy(
            src_ref=stats.at[me],
            dst_ref=stats.at[me],
            send_sem=stat_send.at[b],
            recv_sem=stat_recv.at[me],
            device_id={"seq": b},
            device_id_type=MESH,
        )

    def stat_out(b, carry):
        stat_copy(b).start()
        return carry

    lax.fori_loop(0, me, stat_out, 0)

    def query_side(b, diagonal):
        s = dot(qd[me, 0], kv[b, 0], NT) * scaling
        p = jnp.exp(s - top[:, :1])
        if diagonal:
            r = lax.broadcasted_iota(jnp.int32, (rows, rows), 0)
            c = lax.broadcasted_iota(jnp.int32, (rows, rows), 1)
            p = jnp.where(c <= r, p, 0.0)
        gp = dot(qd[me, 1], kv[b, 1], NT)
        gs = (p * (gp - total[:, :1]) * scaling).astype(jnp.bfloat16)
        return dot(gs, kv[b, 0], NN)

    dq_ref[...] = query_side(me, True)

    def query_step(b, carry):
        dq_ref[...] += query_side(b, False)
        return carry

    lax.fori_loop(0, me, query_step, 0)

    def key_side(b, diagonal):
        s = dot(kv[me, 0], qd[b, 0], NT) * scaling
        p = jnp.exp(s - stats[b, 0:1, :])
        if diagonal:
            r = lax.broadcasted_iota(jnp.int32, (rows, rows), 0)
            c = lax.broadcasted_iota(jnp.int32, (rows, rows), 1)
            p = jnp.where(r <= c, p, 0.0)
        gp = dot(kv[me, 1], qd[b, 1], NT)
        gs = (p * (gp - stats[b, 4:5, :]) * scaling).astype(jnp.bfloat16)
        return dot(gs, qd[b, 0], NN), dot(p.astype(jnp.bfloat16), qd[b, 1], NN)

    dk, dv = key_side(me, True)
    dk_ref[...] = dk
    dv_ref[...] = dv

    def key_step(b, carry):
        @pl.when(lax.rem(b, X) != x)
        def _():
            all_arrived(1, b)

        pltpu.make_async_copy(stats.at[b], stats.at[b], stat_recv.at[b]).wait()
        dk, dv = key_side(b, False)
        dk_ref[...] += dk
        dv_ref[...] += dv
        return carry

    lax.fori_loop(me + 1, S, key_step, 0)

    for copy in swaps:
        copy.wait_send()

    def drain(t, carry):
        for kind in range(2):
            present = (z - t >= 0) if kind == 0 else (z + t < Z)
            for c in range(H):
                for needed, copy in outgoing(kind, t, c):
                    @pl.when(present & needed)
                    def _(copy=copy):
                        copy.wait_send()
        return carry

    lax.fori_loop(0, Z, drain, 0)

    def stat_drain(b, carry):
        stat_copy(b).wait_send()
        return carry

    lax.fori_loop(0, me, stat_drain, 0)


def finish(*refs):
    half = len(refs) // 2
    for source, target in zip(refs[:half], refs[half:]):
        target[...] = source[...]


def solution(mesh):
    S, H = mesh.shape["seq"], mesh.shape["head"]
    X = row_width(S)
    Z = S // X

    def step(queries, keys, values, out_grad):
        rows, width = queries.shape
        f32 = jax.ShapeDtypeStruct((rows, width), jnp.float32)
        DMA = pltpu.SemaphoreType.DMA
        grant = 8 * 2**20 + 16 * S * rows * width
        shapes = (jax.ShapeDtypeStruct((rows, width), jnp.bfloat16), f32, f32, f32)
        results = pl.pallas_call(
            functools.partial(kernel, S, X, H, 1.0 / math.sqrt(width)),
            out_shape=(jax.ShapeDtypeStruct((rows, width), jnp.bfloat16), f32, f32, f32),
            in_specs=[pl.BlockSpec(memory_space=pltpu.HBM)] * 4,
            out_specs=(pl.BlockSpec(memory_space=pltpu.VMEM),) * 4,
            scratch_shapes=[
                pltpu.VMEM((S, 2, rows, width), jnp.bfloat16),
                pltpu.VMEM((S, 2, rows, width), jnp.bfloat16),
                pltpu.VMEM((S, 8, rows), jnp.float32),
                pltpu.VMEM((rows, width), jnp.float32),
                pltpu.VMEM((rows, 128), jnp.float32),
                pltpu.VMEM((rows, 128), jnp.float32),
                DMA((4,)),
                DMA((2, H)),
                DMA((2, H)),
                DMA((2, Z, H)),
                DMA((2, Z, X, H)),
                DMA((2, S, H)),
                DMA((S,)),
                DMA((S,)),
            ],
            compiler_params=pltpu.CompilerParams(collective_id=0, has_side_effects=True, vmem_limit_bytes=grant),
            name="ring_attention",
        )(*(pltpu.with_memory_space_constraint(a, pltpu.HBM) for a in (queries, keys, values, out_grad)))
        return pl.pallas_call(
            finish,
            out_shape=shapes,
            in_specs=[pl.BlockSpec(memory_space=pltpu.VMEM)] * 4,
            out_specs=(pl.BlockSpec(memory_space=pltpu.VMEM),) * 4,
            compiler_params=pltpu.CompilerParams(vmem_limit_bytes=grant),
            name="finish",
        )(*results)

    return jax.shard_map(
        step,
        mesh=mesh,
        in_specs=(
            P("seq", "head"),
            P(("seq", "head"), None),
            P(("seq", "head"), None),
            P("seq", "head"),
        ),
        out_specs=(P("seq", "head"),) * 4,
        check_vma=False,
    )
```
